128 devices in a mesh: tm: 32 (over z, y, core), rep: 4 (over x).
Axes of the slice: x: 4, y: 4, z: 4, core: 2. Of those that a mesh axis runs over, the one named last changes fastest.
Arguments:
- transitions: float32 [128, 512, 512], P(('rep', 'tm')), parts along dimension 0, may hold values from -1 to 1, as said below
- cond_covs: float32 [128, 512, 512], P(('rep', 'tm')), parts along dimension 0, may hold values from -40 to 40, as said below
- transition_est: float32 [2048, 512], P('rep'), parts along dimension 0, may hold values from -0.25 to 0.25
Outputs:
- cov_blocks: float32 [128, 512, 512], P(('rep', 'tm')), parts along dimension 0
- transition_grad: float32 [2048, 512], P('rep'), parts along dimension 0
The draws below stay inside these ranges and needn't reach their ends.
There are 4 independent parts, one for each index of `rep`. The reference program is written for one: setup_inputs(seed, part) draws one part's arguments, and reference() takes and returns one part's arrays. A program takes and returns all parts, laid end to end along the dimension named above; each array names one. Nothing has to cross between parts.
Inputs may be any that keep to these rules, and one draw needn't show every extreme that they name: `transitions`: every block has spectral norm below one. `cond_covs`: every block is symmetric and positive definite.
All inputs are finite; a program needn't handle non-finite values.
Results may differ from the reference program's by a relative error of at most 0.00017.
Values sent between devices are 32-bit elements; how exact they have to be, the bound alone decides.
No kernel may reach another device: no remote copies, remote signals or barrier semaphores. Data moves between devices by JAX's collectives and lax.ppermute only.
A program may use at most 192 MiB of HBM per device.

```python
import math
import jax
import jax.numpy as jnp
from jax import lax

S = 512
EPOCH_TOTAL = 32


def draw_transitions(key, part):
    stochastic_child_keys = jax.random.split(jax.random.fold_in(key, 11), 6)
    fast_share = 0.5
    forgetful = jax.random.uniform(stochastic_child_keys[0], (S,)) < fast_share
    lifetime = jnp.exp(jax.random.uniform(stochastic_child_keys[1], (S,), minval=0.0, maxval=math.log(4.0)))
    fast_retention = jnp.exp(-1.0 / lifetime)
    factor_block = jnp.exp(jax.random.uniform(stochastic_child_keys[2], (EPOCH_TOTAL, 1), minval=math.log(0.5), maxval=math.log(2.0)))
    slow_component_level = jax.random.uniform(stochastic_child_keys[3], (EPOCH_TOTAL, S), minval=0.3, maxval=1.0) * factor_block
    gradual_persistence_weight = 10.0 ** (-slow_component_level / (2.0 * EPOCH_TOTAL))
    perturbation_draws = jax.random.uniform(stochastic_child_keys[4], (EPOCH_TOTAL, 1)) < 3.0 / EPOCH_TOTAL
    gradual_persistence_weight = gradual_persistence_weight * jnp.where(perturbation_draws, 0.7, 1.0)
    persistence_weight = jnp.where(forgetful[None, :], fast_retention[None, :], gradual_persistence_weight)
    mixing = 1.5 * jnp.eye(S, dtype=jnp.float32)[None] + jax.random.normal(stochastic_child_keys[5], (EPOCH_TOTAL, S, S)) / math.sqrt(S)
    orthogonal, upper = jnp.linalg.qr(mixing)
    diagonal_sign = jnp.diagonal(upper, axis1=1, axis2=2)
    diagonal_sign = diagonal_sign / jnp.abs(diagonal_sign)
    orthogonal = orthogonal * diagonal_sign[:, None, :]
    return (persistence_weight[:, :, None] * orthogonal).astype(jnp.float32)


def draw_cond_covs(key, part):
    stochastic_child_keys = jax.random.split(jax.random.fold_in(key, 23), 2)
    factor = jnp.clip(jax.random.normal(stochastic_child_keys[0], (EPOCH_TOTAL, S, S)), -4.0, 4.0)
    wishart = jnp.einsum('bij,bkj->bik', factor, factor, precision=lax.Precision.HIGHEST) / S
    wishart = wishart + 0.5 * jnp.eye(S, dtype=jnp.float32)[None]
    scales = jnp.exp(jax.random.uniform(stochastic_child_keys[1], (EPOCH_TOTAL, S), minval=math.log(0.6), maxval=math.log(1.6)))
    result = scales[:, :, None] * wishart * scales[:, None, :] * (2.0 / math.sqrt(EPOCH_TOTAL))
    return result.astype(jnp.float32)


def scatter_about(key, extent, scale, reach, kind=jnp.bfloat16):
    values = jax.random.normal(key, extent, jnp.float32) * scale
    return jnp.minimum(jnp.maximum(values, -reach), reach).astype(kind)


def setup_inputs(seed: int = 0, part: int = 0) -> dict:
    keys = jax.random.split(jax.random.key(seed), 4)
    part_keys = jax.random.split(jax.random.fold_in(keys[3], part), 4)
    transitions = draw_transitions(jax.random.fold_in(jax.random.fold_in(keys[3], part), 71), part)
    cond_covs = draw_cond_covs(jax.random.fold_in(jax.random.fold_in(keys[3], part), 71), part)
    transition_est = scatter_about(part_keys[2], (S, S), S ** -0.5, 0.25, jnp.float32)
    return dict(transitions=transitions, cond_covs=cond_covs, transition_est=transition_est)


highest = lax.Precision.HIGHEST

def times_transposed(left, right):
    return lax.dot_general(left.astype(jnp.float32), right.astype(jnp.float32), (((1,), (1,)), ((), ())), precision=highest, preferred_element_type=jnp.float32)

def reference(transitions, cond_covs, transition_est):

    def backward_step(covariance, blocks):
        transition, conditional = blocks
        previous_step_cross = times_transposed(covariance, transition)
        current = jnp.dot(transition.astype(jnp.float32), previous_step_cross.astype(jnp.float32), precision=highest, preferred_element_type=jnp.float32) + conditional
        return (current, (current, previous_step_cross))
    empty_block = jnp.zeros((S, S), jnp.float32)
    last_cov, output_values = lax.scan(backward_step, empty_block, (transitions, cond_covs), reverse=True)
    covariances, laggeds = output_values
    lagged_sum = jnp.sum(laggeds[:-1], axis=0)
    variance_accumulator = jnp.sum(covariances[:-1], axis=0)
    gradient = (lagged_sum - jnp.dot(transition_est.astype(jnp.float32), variance_accumulator.astype(jnp.float32), precision=highest, preferred_element_type=jnp.float32)) / (EPOCH_TOTAL - 1)
    return (covariances, gradient)
```

```python
import jax
import jax.numpy as jnp
from jax import lax
from jax.experimental import pallas as pl
from jax.experimental.pallas import tpu as pltpu
from jax.sharding import PartitionSpec as P

ROWS = 4
CHIPS = 4
CORES = 2
PAD = 8
VMEM_LIMIT = 24 * 2**20


def device(z, y, core):
    return ((z % ROWS) * CHIPS + y % CHIPS) * CORES + core


def moved(x, source):
    pairs = []
    for z in range(ROWS):
        for y in range(CHIPS):
            for c in range(CORES):
                origin = source(z, y, c)
                if origin is not None:
                    pairs.append((device(*origin), device(z, y, c)))
    return lax.ppermute(x, "tm", pairs)


def swap_cores(x):
    return moved(x, lambda z, y, c: (z, y, 1 - c))


def from_chip_ahead(x, distance):
    return moved(x, lambda z, y, c: (z, y + distance, c))


def from_row_ahead(x, distance, rows=tuple(range(ROWS))):
    return moved(x, lambda z, y, c: (z + distance, y, c) if z in rows else None)


def place():
    here = lax.axis_index("tm")
    return here // (CHIPS * CORES), (here // CORES) % CHIPS, here % CORES


def split(x):
    high = x.astype(jnp.bfloat16)
    return high, (x - high.astype(jnp.float32)).astype(jnp.bfloat16)


def dot3(left, right, contract=0):
    def one(a, b):
        return lax.dot_general(
            a, b, (((1,), (contract,)), ((), ())), preferred_element_type=jnp.float32
        )

    (left_high, left_low), (right_high, right_low) = left, right
    return one(left_low, right_high) + one(left_high, right_low) + one(left_high, right_high)


def carry(gain, cov, noise):
    return noise + dot3(split(dot3(gain, split(cov))), gain, 1)


def kernel_call(body, shapes, operands, scratch=(), flops=0, moved_bytes=0):
    vmem = pl.BlockSpec(memory_space=pltpu.VMEM)
    return pl.pallas_call(
        body,
        out_shape=[jax.ShapeDtypeStruct(shape, jnp.float32) for shape in shapes],
        in_specs=[vmem] * len(operands),
        out_specs=[vmem] * len(shapes),
        scratch_shapes=[pltpu.VMEM(shape, jnp.float32) for shape in scratch],
        compiler_params=pltpu.CompilerParams(vmem_limit_bytes=VMEM_LIMIT),
        cost_estimate=pl.CostEstimate(flops=flops, bytes_accessed=moved_bytes, transcendentals=0),
    )(*operands)


def rows_at(index, size):
    return pl.ds(pl.multiple_of(index * size, size), size)


def triangles(half):
    rows = lax.broadcasted_iota(jnp.int32, (half, half), 0)
    columns = lax.broadcasted_iota(jnp.int32, (half, half), 1)
    return rows >= columns, rows == columns


def pack(x, out_ref, start, core):
    half = x.shape[0] // 2
    quarter = half // 2
    lower, on_diagonal = triangles(half)
    a, b, d = x[:half, :half], x[:half, half:], x[half:, half:]
    diagonal = jnp.sum(jnp.where(on_diagonal, d, 0.0), axis=0, keepdims=True)
    w = jnp.where(core == 0, jnp.where(lower, a, d), b)
    out_ref[start : start + quarter, :half] = w[:quarter]
    out_ref[start : start + quarter, half:] = w[quarter:]
    out_ref[start + quarter : start + quarter + PAD, :half] = jnp.broadcast_to(diagonal, (PAD, half))
    out_ref[start + quarter : start + quarter + PAD, half:] = jnp.broadcast_to(diagonal, (PAD, half))


def unpack(mine, other, core):
    half = mine.shape[1] // 2
    quarter = half // 2
    lower, on_diagonal = triangles(half)

    def square(x):
        return jnp.concatenate([x[:quarter, :half], x[:quarter, half:]], axis=0)

    diagonal = jnp.where(core == 0, mine, other)[quarter : quarter + 1, :half]
    mine, other = square(mine), square(other)
    w = jnp.where(core == 0, mine, other)
    b = jnp.where(core == 0, other, mine)
    flipped = w.T
    a = jnp.where(lower, w, flipped)
    d = jnp.where(on_diagonal, diagonal, jnp.where(lower, flipped, w))
    top = jnp.concatenate([a, b], axis=1)
    return jnp.concatenate([top, jnp.concatenate([b.T, d], axis=1)], axis=0)


def chip_kernel(gain, gain_other, noise, noise_other, gain_ref, noise_ref, send_ref, g_ref, n_ref):
    _, _, core = place()
    half = gain.shape[0] // 2
    g_ref[core], g_ref[1 - core] = gain[...], gain_other[...]
    n_ref[core], n_ref[1 - core] = noise[...], noise_other[...]
    first = split(g_ref[0])
    gain_ref[...] = dot3(first, split(g_ref[1]))
    send_ref[:half] = gain_ref[rows_at(core, half), :]
    result = carry(first, n_ref[1], n_ref[0])
    noise_ref[...] = result
    pack(result, send_ref, half, core)


def row_kernel(own_gain, own_noise, *refs):
    ahead, ahead_other, behind, behind_other, far, far_other, rest, rest_other = refs[:8]
    after_gain_ref, after_noise_ref, gain_ref, gain_mine_ref, noise_ref, packed_ref, p_ref, n_ref = refs[8:]
    _, y, core = place()
    width = own_gain.shape[0]
    half = width // 2
    p_ref[y], n_ref[y] = own_gain[...], own_noise[...]
    for slot, mine, other in (
        ((y + 1) % CHIPS, ahead, ahead_other),
        ((y + 3) % CHIPS, behind, behind_other),
    ):
        p_ref[slot, rows_at(core, half), :] = mine[:half]
        p_ref[slot, rows_at(1 - core, half), :] = other[:half]
        n_ref[slot] = unpack(mine[half:], other[half:], core)
    slot = (y + 2) % CHIPS
    cut = far.shape[0]
    left = half - cut
    for place_of, upper, lower in ((core, far, rest), (1 - core, far_other, rest_other)):
        start = pl.multiple_of(place_of * half, half)
        p_ref[slot, pl.ds(start, cut), :] = upper[...]
        p_ref[slot, pl.ds(pl.multiple_of(start + cut, 8), left), :] = lower[:left]
    n_ref[slot] = unpack(rest[left:], rest_other[left:], core)

    gain, noise = p_ref[CHIPS - 1], n_ref[CHIPS - 1]

    @pl.when(y == CHIPS - 1)
    def _():
        rows = lax.broadcasted_iota(jnp.int32, (width, width), 0)
        columns = lax.broadcasted_iota(jnp.int32, (width, width), 1)
        after_gain_ref[...] = jnp.where(rows == columns, 1.0, 0.0)
        after_noise_ref[...] = jnp.zeros_like(after_noise_ref)

    for k in range(CHIPS - 2, -1, -1):
        @pl.when(y == k)
        def _(gain=gain, noise=noise):
            after_gain_ref[...] = gain
            after_noise_ref[...] = noise

        step = split(p_ref[k])
        gain = dot3(step, split(gain))
        noise = carry(step, noise, n_ref[k])
    gain_ref[...], noise_ref[...] = gain, noise
    gain_mine_ref[...] = gain_ref[rows_at(core, half), :]
    pack(noise, packed_ref, 0, core)


def after_kernel(
    after_gain, after_noise, gain, gain_other, noise, noise_other, estimate,
    from_gain_ref, from_noise_ref, grad_gain_ref, grad_noise_ref, g_ref, n_ref,
):
    _, _, core = place()

    @pl.when(core == 0)
    def _():
        other = split(gain_other[...])
        g_ref[...] = dot3(other, split(after_gain[...]))
        n_ref[...] = carry(other, after_noise[...], noise_other[...])

    @pl.when(core != 0)
    def _():
        g_ref[...] = after_gain[...]
        n_ref[...] = after_noise[...]

    own, transition = split(gain[...]), split(estimate[...])
    from_gain = dot3(own, split(g_ref[...]))
    from_gain_ref[...] = from_gain
    grad_gain_ref[...] = g_ref[...] - dot3(transition, split(from_gain))
    lagged = dot3(split(n_ref[...]), own, 1)
    from_noise = dot3(own, split(lagged)) + noise[...]
    from_noise_ref[...] = from_noise
    grad_noise_ref[...] = lagged - dot3(transition, split(from_noise))


def next_row_kernel(mine, other, gain, noise, next_ref, packed_ref):
    _, _, core = place()
    following = unpack(mine[...], other[...], core)
    next_ref[...] = following
    pack(carry(split(gain[...]), following, noise[...]), packed_ref, 0, core)


def final_kernel(
    near, near_other, far, far_other, mine, other, following, from_gain, from_noise, grad_gain, grad_noise,
    cov_ref, keep_ref, give_ref, t_ref, g_ref,
):
    z, y, core = place()
    half = mine.shape[0]

    @pl.when(z == 0)
    def _():
        g_ref[rows_at(core, half), :] = mine[...]
        g_ref[rows_at(1 - core, half), :] = other[...]
        second = unpack(far[...], far_other[...], core)
        t_ref[...] = carry(split(g_ref[...]), second, following[...])

    @pl.when(z == 1)
    def _():
        t_ref[...] = unpack(near[...], near_other[...], core)

    @pl.when(z == 2)
    def _():
        t_ref[...] = following[...]

    @pl.when(z == 3)
    def _():
        t_ref[...] = jnp.zeros_like(t_ref)

    gain = split(from_gain[...])
    carried = split(dot3(split(t_ref[...]), gain, 1))
    last = (z == ROWS - 1) & (y == CHIPS - 1) & (core == CORES - 1)
    terms = jnp.where(last, 0.0, grad_noise[...] + dot3(split(grad_gain[...]), carried))
    cov_ref[...] = from_noise[...] + dot3(gain, carried)

    @pl.when(core == 0)
    def _():
        keep_ref[...], give_ref[...] = terms[:half], terms[half:]

    @pl.when(core != 0)
    def _():
        keep_ref[...], give_ref[...] = terms[half:], terms[:half]


def share_kernel(keep, given, *refs):
    outs, total_ref = refs[:CHIPS], refs[CHIPS]
    _, y, _ = place()
    total_ref[...] = keep[...] + given[...]
    for r in range(CHIPS):
        outs[r][...] = total_ref[rows_at((y + r) % CHIPS, outs[r].shape[0]), :]


def sum_kernel(a, b, c, d, out_ref):
    out_ref[...] = (a[...] + b[...]) + (c[...] + d[...])


def total_kernel(count, a, b, c, d, out_ref, z_ref):
    z, _, _ = place()
    for r, piece in enumerate((a, b, c, d)):
        z_ref[(z + r) % ROWS] = piece[...]
    out_ref[...] = ((z_ref[0] + z_ref[1]) + (z_ref[2] + z_ref[3])) / count


def half_kernel(a, b, c, d, out_ref):
    _, y, _ = place()
    for r, piece in enumerate((a, b, c, d)):
        out_ref[rows_at((y + r) % CHIPS, piece.shape[0]), :] = piece[...]


def whole_kernel(mine, other, out_ref):
    _, _, core = place()
    half = mine.shape[0]
    out_ref[rows_at(core, half), :] = mine[...]
    out_ref[rows_at(1 - core, half), :] = other[...]


def on_device(transitions, cond_covs, transition_est):
    gain, noise = transitions[0], cond_covs[0]
    width = gain.shape[0]
    half = width // 2
    square, strip, piece = (width, width), (half, width), (half // 2 + PAD, width)
    chunk = (half // CHIPS, width)
    flops = 6 * width**3
    size = 4 * width * width

    with jax.named_scope("T_chip"):
        gain_other, noise_other = swap_cores(gain), swap_cores(noise)
        chip_gain, chip_noise, mine = kernel_call(
            chip_kernel,
            [square, square, (half + half // 2 + PAD, width)],
            (gain, gain_other, noise, noise_other),
            [(CORES, *square)] * 2,
            3 * flops,
            7 * size,
        )

    with jax.named_scope("T_row"):
        cut = mine.shape[0] // 16 * 8 + 8
        ahead, behind = from_chip_ahead(mine, 1), from_chip_ahead(mine, 3)
        far, rest = from_chip_ahead(ahead[:cut], 1), from_chip_ahead(behind[cut:], 3)
        pieces = []
        for x in (ahead, behind, far, rest):
            pieces += [x, swap_cores(x)]
        after_gain, after_noise, row_gain, row_gain_mine, row_noise, row_packed = kernel_call(
            row_kernel,
            [square, square, square, strip, square, piece],
            (chip_gain, chip_noise, *pieces),
            [(CHIPS, *square)] * 2,
            9 * flops,
            13 * size,
        )

    with jax.named_scope("T_z"):
        next_mine = from_row_ahead(row_packed, 1, (0, 2))
        gain_mine = from_row_ahead(row_gain_mine, 1, (0,))
        parts = kernel_call(
            after_kernel,
            [square] * 4,
            (after_gain, after_noise, gain, gain_other, noise, noise_other, transition_est),
            [square] * 2,
            8 * flops,
            11 * size,
        )
        next_mine, *parts = lax.optimization_barrier((next_mine, *parts))
        from_gain, from_noise, grad_gain, grad_noise = parts
        next_noise, second_packed = kernel_call(
            next_row_kernel,
            [square, piece],
            (next_mine, swap_cores(next_mine), row_gain, row_noise),
            (),
            2 * flops,
            4 * size,
        )
        near, far = from_row_ahead(second_packed, 1, (1,)), from_row_ahead(second_packed, 2, (0,))
        covariance, keep, give = kernel_call(
            final_kernel,
            [square, strip, strip],
            (
                near, swap_cores(near), far, swap_cores(far), gain_mine, swap_cores(gain_mine), next_noise,
                from_gain, from_noise, grad_gain, grad_noise,
            ),
            [square] * 2,
            5 * flops,
            10 * size,
        )

    with jax.named_scope("T_reduce"):
        own, *sent = kernel_call(
            share_kernel, [chunk] * CHIPS, (keep, swap_cores(give)), [strip], size // 4, size
        )
        received = [from_chip_ahead(sent[r - 1], CHIPS - r) for r in (1, 2, 3)]
        (row_sum,) = kernel_call(sum_kernel, [chunk], (own, *received), (), size // 8, size)
        received = [from_row_ahead(row_sum, r) for r in (1, 2, 3)]
        terms = lax.axis_size("tm") - 1
        (total,) = kernel_call(
            lambda *refs: total_kernel(terms, *refs),
            [chunk],
            (row_sum, *received),
            [(ROWS, *chunk)],
            size // 8,
            size,
        )
        received = [from_chip_ahead(total, r) for r in (1, 2, 3)]
        (gradient_mine,) = kernel_call(half_kernel, [strip], (total, *received), (), size // 8, size)
        (gradient,) = kernel_call(
            whole_kernel, [square], (gradient_mine, swap_cores(gradient_mine)), (), size // 4, 2 * size
        )
    return covariance[None], gradient


def solution(mesh):
    return jax.shard_map(
        on_device,
        mesh=mesh,
        in_specs=(P(("rep", "tm"), None, None), P(("rep", "tm"), None, None), P("rep", None)),
        out_specs=(P(("rep", "tm"), None, None), P("rep", None)),
        check_vma=False,
    )
```

```python
import jax
import jax.numpy as jnp
from jax import lax
from jax.experimental import pallas as pl
from jax.experimental.pallas import tpu as pltpu
from jax.sharding import PartitionSpec as P

ROWS = 4
CHIPS = 4
CORES = 2
PAD = 8
VMEM_LIMIT = 24 * 2**20


def device(z, y, core):
    return ((z % ROWS) * CHIPS + y % CHIPS) * CORES + core


def moved(x, source):
    pairs = []
    for z in range(ROWS):
        for y in range(CHIPS):
            for c in range(CORES):
                origin = source(z, y, c)
                if origin is not None:
                    pairs.append((device(*origin), device(z, y, c)))
    return lax.ppermute(x, "tm", pairs)


def swap_cores(x):
    return moved(x, lambda z, y, c: (z, y, 1 - c))


def from_chip_ahead(x, distance):
    return moved(x, lambda z, y, c: (z, y + distance, c))


def from_row_ahead(x, distance, rows=tuple(range(ROWS))):
    return moved(x, lambda z, y, c: (z + distance, y, c) if z in rows else None)


def place():
    here = lax.axis_index("tm")
    return here // (CHIPS * CORES), (here // CORES) % CHIPS, here % CORES


def split(x):
    high = x.astype(jnp.bfloat16)
    return high, (x - high.astype(jnp.float32)).astype(jnp.bfloat16)


def dot3(left, right, contract=0):
    def one(a, b):
        return lax.dot_general(
            a, b, (((1,), (contract,)), ((), ())), preferred_element_type=jnp.float32
        )

    (left_high, left_low), (right_high, right_low) = left, right
    return one(left_low, right_high) + one(left_high, right_low) + one(left_high, right_high)


def carry(gain, cov, noise):
    return noise + dot3(split(dot3(gain, split(cov))), gain, 1)


def kernel_call(body, shapes, operands, scratch=(), flops=0, moved_bytes=0, in_hbm=0):
    vmem, hbm = pl.BlockSpec(memory_space=pltpu.VMEM), pl.BlockSpec(memory_space=pltpu.HBM)
    semaphores = [pltpu.SemaphoreType.DMA((in_hbm,))] if in_hbm else []
    return pl.pallas_call(
        body,
        out_shape=[
            jax.ShapeDtypeStruct(shape, jnp.float32) if type(shape) is tuple else shape for shape in shapes
        ],
        in_specs=[hbm] * in_hbm + [vmem] * (len(operands) - in_hbm),
        out_specs=[vmem] * len(shapes),
        scratch_shapes=[pltpu.VMEM(shape, jnp.float32) for shape in scratch] + semaphores,
        compiler_params=pltpu.CompilerParams(vmem_limit_bytes=VMEM_LIMIT),
        cost_estimate=pl.CostEstimate(flops=flops, bytes_accessed=moved_bytes, transcendentals=0),
    )(*operands)


def rows_at(index, size):
    return pl.ds(pl.multiple_of(index * size, size), size)


def triangles(half):
    rows = lax.broadcasted_iota(jnp.int32, (half, half), 0)
    columns = lax.broadcasted_iota(jnp.int32, (half, half), 1)
    return rows >= columns, rows == columns


def pack(x, out_ref, start, core):
    half = x.shape[0] // 2
    quarter = half // 2
    lower, on_diagonal = triangles(half)
    a, b, d = x[:half, :half], x[:half, half:], x[half:, half:]
    diagonal = jnp.sum(jnp.where(on_diagonal, d, 0.0), axis=0, keepdims=True)
    w = jnp.where(core == 0, jnp.where(lower, a, d), b)
    out_ref[start : start + quarter, :half] = w[:quarter]
    out_ref[start : start + quarter, half:] = w[quarter:]
    out_ref[start + quarter : start + quarter + PAD, :half] = jnp.broadcast_to(diagonal, (PAD, half))
    out_ref[start + quarter : start + quarter + PAD, half:] = jnp.broadcast_to(diagonal, (PAD, half))


def unpack(mine, other, core):
    half = mine.shape[1] // 2
    quarter = half // 2
    lower, on_diagonal = triangles(half)

    def square(x):
        return jnp.concatenate([x[:quarter, :half], x[:quarter, half:]], axis=0)

    diagonal = jnp.where(core == 0, mine, other)[quarter : quarter + 1, :half]
    mine, other = square(mine), square(other)
    w = jnp.where(core == 0, mine, other)
    b = jnp.where(core == 0, other, mine)
    flipped = w.T
    a = jnp.where(lower, w, flipped)
    d = jnp.where(on_diagonal, diagonal, jnp.where(lower, flipped, w))
    top = jnp.concatenate([a, b], axis=1)
    return jnp.concatenate([top, jnp.concatenate([b.T, d], axis=1)], axis=0)


def chip_gain_kernel(gain, gain_other, gain_ref, send_ref, g_ref, sems):
    _, _, core = place()
    copy = pltpu.make_async_copy(gain, g_ref.at[core], sems.at[0])
    copy.start()
    g_ref[1 - core] = gain_other[...]
    copy.wait()
    gain_ref[...] = dot3(split(g_ref[0]), split(g_ref[1]))
    send_ref[...] = gain_ref[rows_at(core, send_ref.shape[0]), :]


def chip_noise_kernel(gain, noise, gain_other, noise_other, noise_ref, packed_ref, g_ref, n_ref, sems):
    _, _, core = place()
    copies = [
        pltpu.make_async_copy(gain, g_ref.at[core], sems.at[0]),
        pltpu.make_async_copy(noise, n_ref.at[core], sems.at[1]),
    ]
    for copy in copies:
        copy.start()
    g_ref[1 - core], n_ref[1 - core] = gain_other[...], noise_other[...]
    for copy in copies:
        copy.wait()
    result = carry(split(g_ref[0]), n_ref[1], n_ref[0])
    noise_ref[...] = result
    pack(result, packed_ref, 0, core)


def row_gains_kernel(own, *refs):
    ahead, ahead_other, behind, behind_other, far, far_other, rest, rest_other = refs[:8]
    high_ref, low_ref, after_ref, row_ref, mine_ref, p_ref = refs[8:]
    _, y, core = place()
    width = own.shape[0]
    half = width // 2
    p_ref[y] = own[...]
    for slot, mine, other in (
        ((y + 1) % CHIPS, ahead, ahead_other),
        ((y + 3) % CHIPS, behind, behind_other),
    ):
        p_ref[slot, rows_at(core, half), :] = mine[...]
        p_ref[slot, rows_at(1 - core, half), :] = other[...]
    slot = (y + 2) % CHIPS
    cut = half // 2
    for place_of, upper, lower in ((core, far, rest), (1 - core, far_other, rest_other)):
        p_ref[slot, rows_at(2 * place_of, cut), :] = upper[:cut]
        p_ref[slot, rows_at(2 * place_of + 1, cut), :] = lower[:cut]

    gain = p_ref[CHIPS - 1]

    @pl.when(y == CHIPS - 1)
    def _():
        rows = lax.broadcasted_iota(jnp.int32, (width, width), 0)
        columns = lax.broadcasted_iota(jnp.int32, (width, width), 1)
        after_ref[...] = jnp.where(rows == columns, 1.0, 0.0)

    for k in range(CHIPS - 2, -1, -1):
        @pl.when(y == k)
        def _(gain=gain):
            after_ref[...] = gain

        step = split(p_ref[k])
        high_ref[k], low_ref[k] = step
        gain = dot3(step, split(gain))
    row_ref[...] = gain
    mine_ref[...] = row_ref[rows_at(core, half), :]


def row_noises_kernel(high_ref, low_ref, own, *refs):
    ahead, ahead_other, behind, behind_other, far, far_other, rest, rest_other = refs[:8]
    after_ref, noise_ref, packed_ref, n_ref = refs[8:]
    _, y, core = place()
    n_ref[y] = own[...]
    n_ref[(y + 1) % CHIPS] = unpack(ahead[...], ahead_other[...], core)
    n_ref[(y + 3) % CHIPS] = unpack(behind[...], behind_other[...], core)
    cut = own.shape[0] // 4
    n_ref[(y + 2) % CHIPS] = unpack(
        jnp.concatenate([far[cut:], rest[cut:]], axis=0),
        jnp.concatenate([far_other[cut:], rest_other[cut:]], axis=0),
        core,
    )
    noise = n_ref[CHIPS - 1]

    @pl.when(y == CHIPS - 1)
    def _():
        after_ref[...] = jnp.zeros_like(after_ref)

    for k in range(CHIPS - 2, -1, -1):
        @pl.when(y == k)
        def _(noise=noise):
            after_ref[...] = noise

        noise = carry((high_ref[k], low_ref[k]), noise, n_ref[k])
    noise_ref[...] = noise
    pack(noise, packed_ref, 0, core)


def after_kernel(
    after_gain, after_noise, gain, gain_other, noise, noise_other, estimate,
    from_gain_ref, from_noise_ref, grad_gain_ref, grad_noise_ref, g_ref, n_ref,
):
    _, _, core = place()

    @pl.when(core == 0)
    def _():
        other = split(gain_other[...])
        g_ref[...] = dot3(other, split(after_gain[...]))
        n_ref[...] = carry(other, after_noise[...], noise_other[...])

    @pl.when(core != 0)
    def _():
        g_ref[...] = after_gain[...]
        n_ref[...] = after_noise[...]

    own, transition = split(gain[...]), split(estimate[...])
    from_gain = dot3(own, split(g_ref[...]))
    from_gain_ref[...] = from_gain
    grad_gain_ref[...] = g_ref[...] - dot3(transition, split(from_gain))
    lagged = dot3(split(n_ref[...]), own, 1)
    from_noise = dot3(own, split(lagged)) + noise[...]
    from_noise_ref[...] = from_noise
    grad_noise_ref[...] = lagged - dot3(transition, split(from_noise))


def next_row_kernel(mine, other, gain, noise, next_ref, packed_ref):
    _, _, core = place()
    following = unpack(mine[...], other[...], core)
    next_ref[...] = following
    pack(carry(split(gain[...]), following, noise[...]), packed_ref, 0, core)


def final_kernel(
    near, near_other, far, far_other, lead, lead_other, first, first_other, following, from_gain, grad_gain, grad_noise,
    carried_ref, keep_ref, give_ref, t_ref, g_ref,
):
    z, y, core = place()
    half = keep_ref.shape[0]

    @pl.when(z == 0)
    def _():
        g_ref[rows_at(core, half), :] = lead[...]
        g_ref[rows_at(1 - core, half), :] = lead_other[...]
        second = unpack(far[...], far_other[...], core)
        t_ref[...] = carry(split(g_ref[...]), second, unpack(first[...], first_other[...], core))

    @pl.when(z == 1)
    def _():
        t_ref[...] = unpack(near[...], near_other[...], core)

    @pl.when(z == 2)
    def _():
        t_ref[...] = following[...]

    @pl.when(z == 3)
    def _():
        t_ref[...] = jnp.zeros_like(t_ref)

    gain = split(from_gain[...])
    carried_ref[...] = dot3(split(t_ref[...]), gain, 1)
    carried = split(carried_ref[...])
    last = (z == ROWS - 1) & (y == CHIPS - 1) & (core == CORES - 1)
    terms = jnp.where(last, 0.0, grad_noise[...] + dot3(split(grad_gain[...]), carried))

    @pl.when(core == 0)
    def _():
        keep_ref[...], give_ref[...] = terms[:half], terms[half:]

    @pl.when(core != 0)
    def _():
        keep_ref[...], give_ref[...] = terms[half:], terms[:half]


def covariance_kernel(from_gain, from_noise, carried, out_ref):
    out_ref[...] = from_noise[...] + dot3(split(from_gain[...]), split(carried[...]))


def share_kernel(keep, given, out_ref):
    out_ref[...] = (keep[...] + given[...]).reshape(out_ref.shape)


def sum_kernel(count, pieces, out_ref):
    total = pieces[0]
    for k in range(1, pieces.shape[0]):
        total = total + pieces[k]
    total = total / count
    for k in range(pieces.shape[0]):
        out_ref[k] = total


def whole_kernel(mine, other, out_ref):
    _, _, core = place()
    half = mine.shape[0]
    out_ref[rows_at(core, half), :] = mine[...]
    out_ref[rows_at(1 - core, half), :] = other[...]


def on_device(transitions, cond_covs, transition_est):
    gain, noise = transitions[0], cond_covs[0]
    width = gain.shape[0]
    half = width // 2
    square, strip, piece = (width, width), (half, width), (half // 2 + PAD, width)
    groups = [[device(z, y, c) for z in range(ROWS) for y in range(CHIPS)] for c in range(CORES)]
    spread = (ROWS * CHIPS, half // (ROWS * CHIPS), width)
    flops = 6 * width**3
    size = 4 * width * width

    three = jax.ShapeDtypeStruct((CHIPS - 1, *square), jnp.bfloat16)

    with jax.named_scope("T_chip"):
        gain_other, noise_other = swap_cores(gain), swap_cores(noise)
        chip_gain, gain_mine = kernel_call(
            chip_gain_kernel, [square, strip], (gain, gain_other), [(CORES, *square)], flops, 4 * size, 1
        )
        chip_noise, noise_mine = kernel_call(
            chip_noise_kernel,
            [square, piece],
            (gain, noise, gain_other, noise_other),
            [(CORES, *square)] * 2,
            2 * flops,
            6 * size,
            2,
        )

    with jax.named_scope("T_row"):
        gains = [from_chip_ahead(gain_mine, r) for r in (1, 3)]
        noises = [from_chip_ahead(noise_mine, r) for r in (1, 3)]
        cut, cut_noise = half // 2, (piece[0] // 2 + PAD - 1) // PAD * PAD
        far = from_chip_ahead(jnp.concatenate([gains[0][:cut], noises[0][:cut_noise]], axis=0), 1)
        rest = from_chip_ahead(jnp.concatenate([gains[1][cut:], noises[1][cut_noise:]], axis=0), 3)
        gain_pieces, noise_pieces = [], []
        for x in (*gains, far, rest):
            gain_pieces += [x, swap_cores(x)]
        for x in noises:
            noise_pieces += [x, swap_cores(x)]
        high, low, after_gain, row_gain, row_gain_mine = kernel_call(
            row_gains_kernel,
            [three, three, square, square, strip],
            (chip_gain, *gain_pieces),
            [(CHIPS, *square)],
            3 * flops,
            10 * size,
        )
        after_noise, row_noise, row_packed = kernel_call(
            row_noises_kernel,
            [square, square, piece],
            (high, low, chip_noise, *noise_pieces, *gain_pieces[4:]),
            [(CHIPS, *square)],
            6 * flops,
            8 * size,
        )

    with jax.named_scope("T_z"):
        next_mine = from_row_ahead(row_packed, 1, (2,))
        leads = [from_row_ahead(x, 1, (0,)) for x in (row_gain_mine, row_packed)]
        parts = kernel_call(
            after_kernel,
            [square] * 4,
            (after_gain, after_noise, gain, gain_other, noise, noise_other, transition_est),
            [square] * 2,
            8 * flops,
            11 * size,
        )
        next_mine, *parts = lax.optimization_barrier((next_mine, *parts))
        from_gain, from_noise, grad_gain, grad_noise = parts
        next_noise, second_packed = kernel_call(
            next_row_kernel,
            [square, piece],
            (next_mine, swap_cores(next_mine), row_gain, row_noise),
            (),
            2 * flops,
            4 * size,
        )
        near, far = from_row_ahead(second_packed, 1, (1,)), from_row_ahead(second_packed, 2, (0,))
        carried, keep, give = kernel_call(
            final_kernel,
            [square, strip, strip],
            (
                near, swap_cores(near), far, swap_cores(far), leads[0], swap_cores(leads[0]), leads[1], swap_cores(leads[1]), next_noise,
                from_gain, grad_gain, grad_noise,
            ),
            [square] * 2,
            4 * flops,
            10 * size,
        )

        (covariance,) = kernel_call(
            covariance_kernel, [square], (from_gain, from_noise, carried), (), flops, 4 * size
        )

    with jax.named_scope("T_reduce"):
        (pieces,) = kernel_call(share_kernel, [spread], (keep, swap_cores(give)), (), size // 4, size)
        pieces = lax.all_to_all(pieces, "tm", 0, 0, axis_index_groups=groups)
        terms = lax.axis_size("tm") - 1
        (pieces,) = kernel_call(
            lambda *refs: sum_kernel(terms, *refs), [spread], (pieces,), (), size // 4, size
        )
        pieces = lax.all_to_all(pieces, "tm", 0, 0, axis_index_groups=groups)
        gradient_mine = pieces.reshape(strip)
        (gradient,) = kernel_call(
            whole_kernel, [square], (gradient_mine, swap_cores(gradient_mine)), (), size // 4, 2 * size
        )
    return covariance[None], gradient


def solution(mesh):
    return jax.shard_map(
        on_device,
        mesh=mesh,
        in_specs=(P(("rep", "tm"), None, None), P(("rep", "tm"), None, None), P("rep", None)),
        out_specs=(P(("rep", "tm"), None, None), P("rep", None)),
        check_vma=False,
    )
```

```python
import jax
import jax.numpy as jnp
from jax import lax
from jax.experimental import pallas as pl
from jax.experimental.pallas import tpu as pltpu
from jax.sharding import PartitionSpec as P

ROWS = 4
CHIPS = 4
CORES = 2
PAD = 8
VMEM_LIMIT = 24 * 2**20


def device(z, y, core):
    return ((z % ROWS) * CHIPS + y % CHIPS) * CORES + core


def moved(x, source):
    pairs = []
    for z in range(ROWS):
        for y in range(CHIPS):
            for c in range(CORES):
                origin = source(z, y, c)
                if origin is not None:
                    pairs.append((device(*origin), device(z, y, c)))
    return lax.ppermute(x, "tm", pairs)


def swap_cores(x):
    return moved(x, lambda z, y, c: (z, y, 1 - c))


def from_chip_ahead(x, distance):
    return moved(x, lambda z, y, c: (z, y + distance, c))


def from_row_ahead(x, distance, rows=tuple(range(ROWS))):
    return moved(x, lambda z, y, c: (z + distance, y, c) if z in rows else None)


def place():
    here = lax.axis_index("tm")
    return here // (CHIPS * CORES), (here // CORES) % CHIPS, here % CORES


def split(x):
    high = x.astype(jnp.bfloat16)
    return high, (x - high.astype(jnp.float32)).astype(jnp.bfloat16)


def dot3(left, right, contract=0):
    def one(a, b):
        return lax.dot_general(
            a, b, (((1,), (contract,)), ((), ())), preferred_element_type=jnp.float32
        )

    (left_high, left_low), (right_high, right_low) = left, right
    return one(left_low, right_high) + one(left_high, right_low) + one(left_high, right_high)


def carry(gain, cov, noise):
    return noise + dot3(split(dot3(gain, split(cov))), gain, 1)


def kernel_call(body, shapes, operands, scratch=(), flops=0, moved_bytes=0, in_hbm=0):
    vmem, hbm = pl.BlockSpec(memory_space=pltpu.VMEM), pl.BlockSpec(memory_space=pltpu.HBM)
    semaphores = [pltpu.SemaphoreType.DMA((in_hbm,))] if in_hbm else []
    return pl.pallas_call(
        body,
        out_shape=[
            jax.ShapeDtypeStruct(shape, jnp.float32) if type(shape) is tuple else shape for shape in shapes
        ],
        in_specs=[hbm] * in_hbm + [vmem] * (len(operands) - in_hbm),
        out_specs=[vmem] * len(shapes),
        scratch_shapes=[pltpu.VMEM(shape, jnp.float32) for shape in scratch] + semaphores,
        compiler_params=pltpu.CompilerParams(vmem_limit_bytes=VMEM_LIMIT),
        cost_estimate=pl.CostEstimate(flops=flops, bytes_accessed=moved_bytes, transcendentals=0),
    )(*operands)


def rows_at(index, size):
    return pl.ds(pl.multiple_of(index * size, size), size)


def triangles(half):
    rows = lax.broadcasted_iota(jnp.int32, (half, half), 0)
    columns = lax.broadcasted_iota(jnp.int32, (half, half), 1)
    return rows >= columns, rows == columns


def pack(x, out_ref, start, core):
    half = x.shape[0] // 2
    quarter = half // 2
    lower, on_diagonal = triangles(half)
    a, b, d = x[:half, :half], x[:half, half:], x[half:, half:]
    diagonal = jnp.sum(jnp.where(on_diagonal, d, 0.0), axis=0, keepdims=True)
    w = jnp.where(core == 0, jnp.where(lower, a, d), b)
    out_ref[start : start + quarter, :half] = w[:quarter]
    out_ref[start : start + quarter, half:] = w[quarter:]
    out_ref[start + quarter : start + quarter + PAD, :half] = jnp.broadcast_to(diagonal, (PAD, half))
    out_ref[start + quarter : start + quarter + PAD, half:] = jnp.broadcast_to(diagonal, (PAD, half))


def unpack(mine, other, core):
    half = mine.shape[1] // 2
    quarter = half // 2
    lower, on_diagonal = triangles(half)

    def square(x):
        return jnp.concatenate([x[:quarter, :half], x[:quarter, half:]], axis=0)

    diagonal = jnp.where(core == 0, mine, other)[quarter : quarter + 1, :half]
    mine, other = square(mine), square(other)
    w = jnp.where(core == 0, mine, other)
    b = jnp.where(core == 0, other, mine)
    flipped = w.T
    a = jnp.where(lower, w, flipped)
    d = jnp.where(on_diagonal, diagonal, jnp.where(lower, flipped, w))
    top = jnp.concatenate([a, b], axis=1)
    return jnp.concatenate([top, jnp.concatenate([b.T, d], axis=1)], axis=0)


def copy_kernel(gain, noise, gain_ref, noise_ref):
    gain_ref[...], noise_ref[...] = gain[...], noise[...]


def chip_gain_kernel(gain, gain_other, gain_ref, send_ref, g_ref):
    _, _, core = place()
    g_ref[core], g_ref[1 - core] = gain[...], gain_other[...]
    gain_ref[...] = dot3(split(g_ref[0]), split(g_ref[1]))
    send_ref[...] = gain_ref[rows_at(core, send_ref.shape[0]), :]


def chip_noise_kernel(gain, noise, gain_other, noise_other, noise_ref, packed_ref, g_ref, n_ref):
    _, _, core = place()
    g_ref[core], g_ref[1 - core] = gain[...], gain_other[...]
    n_ref[core], n_ref[1 - core] = noise[...], noise_other[...]
    result = carry(split(g_ref[0]), n_ref[1], n_ref[0])
    noise_ref[...] = result
    pack(result, packed_ref, 0, core)


def row_gains_kernel(own, *refs):
    ahead, ahead_other, behind, behind_other, far, far_other, rest, rest_other = refs[:8]
    high_ref, low_ref, after_ref, row_ref, mine_ref, p_ref = refs[8:]
    _, y, core = place()
    width = own.shape[0]
    half = width // 2
    p_ref[y] = own[...]
    for slot, mine, other in (
        ((y + 1) % CHIPS, ahead, ahead_other),
        ((y + 3) % CHIPS, behind, behind_other),
    ):
        p_ref[slot, rows_at(core, half), :] = mine[...]
        p_ref[slot, rows_at(1 - core, half), :] = other[...]
    slot = (y + 2) % CHIPS
    cut = half // 2
    for place_of, upper, lower in ((core, far, rest), (1 - core, far_other, rest_other)):
        p_ref[slot, rows_at(2 * place_of, cut), :] = upper[:cut]
        p_ref[slot, rows_at(2 * place_of + 1, cut), :] = lower[:cut]

    gain = p_ref[CHIPS - 1]

    @pl.when(y == CHIPS - 1)
    def _():
        rows = lax.broadcasted_iota(jnp.int32, (width, width), 0)
        columns = lax.broadcasted_iota(jnp.int32, (width, width), 1)
        after_ref[...] = jnp.where(rows == columns, 1.0, 0.0)

    for k in range(CHIPS - 2, -1, -1):
        @pl.when(y == k)
        def _(gain=gain):
            after_ref[...] = gain

        step = split(p_ref[k])
        high_ref[k], low_ref[k] = step
        gain = dot3(step, split(gain))
    row_ref[...] = gain
    mine_ref[...] = row_ref[rows_at(core, half), :]


def row_noises_kernel(high_ref, low_ref, own, *refs):
    ahead, ahead_other, behind, behind_other, far, far_other, rest, rest_other = refs[:8]
    after_ref, noise_ref, packed_ref, n_ref = refs[8:]
    _, y, core = place()
    n_ref[y] = own[...]
    n_ref[(y + 1) % CHIPS] = unpack(ahead[...], ahead_other[...], core)
    n_ref[(y + 3) % CHIPS] = unpack(behind[...], behind_other[...], core)
    cut = own.shape[0] // 4
    n_ref[(y + 2) % CHIPS] = unpack(
        jnp.concatenate([far[cut:], rest[cut:]], axis=0),
        jnp.concatenate([far_other[cut:], rest_other[cut:]], axis=0),
        core,
    )
    noise = n_ref[CHIPS - 1]

    @pl.when(y == CHIPS - 1)
    def _():
        after_ref[...] = jnp.zeros_like(after_ref)

    for k in range(CHIPS - 2, -1, -1):
        @pl.when(y == k)
        def _(noise=noise):
            after_ref[...] = noise

        noise = carry((high_ref[k], low_ref[k]), noise, n_ref[k])
    noise_ref[...] = noise
    pack(noise, packed_ref, 0, core)


def after_kernel(
    after_gain, after_noise, gain, gain_other, noise, noise_other, estimate,
    from_gain_ref, from_noise_ref, grad_gain_ref, grad_noise_ref, g_ref, n_ref,
):
    _, _, core = place()

    @pl.when(core == 0)
    def _():
        other = split(gain_other[...])
        g_ref[...] = dot3(other, split(after_gain[...]))
        n_ref[...] = carry(other, after_noise[...], noise_other[...])

    @pl.when(core != 0)
    def _():
        g_ref[...] = after_gain[...]
        n_ref[...] = after_noise[...]

    own, transition = split(gain[...]), split(estimate[...])
    from_gain = dot3(own, split(g_ref[...]))
    from_gain_ref[...] = from_gain
    grad_gain_ref[...] = g_ref[...] - dot3(transition, split(from_gain))
    lagged = dot3(split(n_ref[...]), own, 1)
    from_noise = dot3(own, split(lagged)) + noise[...]
    from_noise_ref[...] = from_noise
    grad_noise_ref[...] = lagged - dot3(transition, split(from_noise))


def next_row_kernel(mine, other, gain, noise, next_ref, packed_ref):
    _, _, core = place()
    following = unpack(mine[...], other[...], core)
    next_ref[...] = following
    pack(carry(split(gain[...]), following, noise[...]), packed_ref, 0, core)


def final_kernel(
    near, near_other, far, far_other, lead, lead_other, first, first_other, following, from_gain, grad_gain, grad_noise,
    carried_ref, keep_ref, give_ref, t_ref, g_ref,
):
    z, y, core = place()
    half = keep_ref.shape[0]

    @pl.when(z == 0)
    def _():
        g_ref[rows_at(core, half), :] = lead[...]
        g_ref[rows_at(1 - core, half), :] = lead_other[...]
        second = unpack(far[...], far_other[...], core)
        t_ref[...] = carry(split(g_ref[...]), second, unpack(first[...], first_other[...], core))

    @pl.when(z == 1)
    def _():
        t_ref[...] = unpack(near[...], near_other[...], core)

    @pl.when(z == 2)
    def _():
        t_ref[...] = following[...]

    @pl.when(z == 3)
    def _():
        t_ref[...] = jnp.zeros_like(t_ref)

    gain = split(from_gain[...])
    carried_ref[...] = dot3(split(t_ref[...]), gain, 1)
    carried = split(carried_ref[...])
    last = (z == ROWS - 1) & (y == CHIPS - 1) & (core == CORES - 1)
    terms = jnp.where(last, 0.0, grad_noise[...] + dot3(split(grad_gain[...]), carried))

    @pl.when(core == 0)
    def _():
        keep_ref[...], give_ref[...] = terms[:half], terms[half:]

    @pl.when(core != 0)
    def _():
        keep_ref[...], give_ref[...] = terms[half:], terms[:half]


def covariance_kernel(from_gain, from_noise, carried, out_ref):
    out_ref[...] = from_noise[...] + dot3(split(from_gain[...]), split(carried[...]))


def share_kernel(keep, given, out_ref):
    out_ref[...] = (keep[...] + given[...]).reshape(out_ref.shape)


def sum_kernel(count, pieces, out_ref):
    total = pieces[0]
    for k in range(1, pieces.shape[0]):
        total = total + pieces[k]
    total = total / count
    for k in range(pieces.shape[0]):
        out_ref[k] = total


def whole_kernel(mine, other, out_ref):
    _, _, core = place()
    half = mine.shape[0]
    out_ref[rows_at(core, half), :] = mine[...]
    out_ref[rows_at(1 - core, half), :] = other[...]


def on_device(transitions, cond_covs, transition_est):
    gain, noise = transitions[0], cond_covs[0]
    width = gain.shape[0]
    half = width // 2
    square, strip, piece = (width, width), (half, width), (half // 2 + PAD, width)
    groups = [[device(z, y, c) for z in range(ROWS) for y in range(CHIPS)] for c in range(CORES)]
    spread = (ROWS * CHIPS, half // (ROWS * CHIPS), width)
    flops = 6 * width**3
    size = 4 * width * width

    three = jax.ShapeDtypeStruct((CHIPS - 1, *square), jnp.bfloat16)

    with jax.named_scope("T_chip"):
        gain_other, noise_other = swap_cores(gain), swap_cores(noise)
        gain, noise = kernel_call(copy_kernel, [square] * 2, (gain, noise), (), 0, 4 * size)
        chip_gain, gain_mine = kernel_call(
            chip_gain_kernel, [square, strip], (gain, gain_other), [(CORES, *square)], flops, 4 * size
        )
        chip_noise, noise_mine = kernel_call(
            chip_noise_kernel,
            [square, piece],
            (gain, noise, gain_other, noise_other),
            [(CORES, *square)] * 2,
            2 * flops,
            6 * size,
        )

    with jax.named_scope("T_row"):
        gains = [from_chip_ahead(gain_mine, r) for r in (1, 3)]
        noises = [from_chip_ahead(noise_mine, r) for r in (1, 3)]
        cut, cut_noise = half // 2, (piece[0] // 2 + PAD - 1) // PAD * PAD
        far = from_chip_ahead(jnp.concatenate([gains[0][:cut], noises[0][:cut_noise]], axis=0), 1)
        rest = from_chip_ahead(jnp.concatenate([gains[1][cut:], noises[1][cut_noise:]], axis=0), 3)
        gain_pieces, noise_pieces = [], []
        for x in (*gains, far, rest):
            gain_pieces += [x, swap_cores(x)]
        for x in noises:
            noise_pieces += [x, swap_cores(x)]
        high, low, after_gain, row_gain, row_gain_mine = kernel_call(
            row_gains_kernel,
            [three, three, square, square, strip],
            (chip_gain, *gain_pieces),
            [(CHIPS, *square)],
            3 * flops,
            10 * size,
        )
        after_noise, row_noise, row_packed = kernel_call(
            row_noises_kernel,
            [square, square, piece],
            (high, low, chip_noise, *noise_pieces, *gain_pieces[4:]),
            [(CHIPS, *square)],
            6 * flops,
            8 * size,
        )

    with jax.named_scope("T_z"):
        next_mine = from_row_ahead(row_packed, 1, (2,))
        leads = [from_row_ahead(x, 1, (0,)) for x in (row_gain_mine, row_packed)]
        parts = kernel_call(
            after_kernel,
            [square] * 4,
            (after_gain, after_noise, gain, gain_other, noise, noise_other, transition_est),
            [square] * 2,
            8 * flops,
            11 * size,
        )
        next_mine, *parts = lax.optimization_barrier((next_mine, *parts))
        from_gain, from_noise, grad_gain, grad_noise = parts
        next_noise, second_packed = kernel_call(
            next_row_kernel,
            [square, piece],
            (next_mine, swap_cores(next_mine), row_gain, row_noise),
            (),
            2 * flops,
            4 * size,
        )
        near, far = from_row_ahead(second_packed, 1, (1,)), from_row_ahead(second_packed, 2, (0,))
        carried, keep, give = kernel_call(
            final_kernel,
            [square, strip, strip],
            (
                near, swap_cores(near), far, swap_cores(far), leads[0], swap_cores(leads[0]), leads[1], swap_cores(leads[1]), next_noise,
                from_gain, grad_gain, grad_noise,
            ),
            [square] * 2,
            4 * flops,
            10 * size,
        )

        (covariance,) = kernel_call(
            covariance_kernel, [square], (from_gain, from_noise, carried), (), flops, 4 * size
        )

    with jax.named_scope("T_reduce"):
        (pieces,) = kernel_call(share_kernel, [spread], (keep, swap_cores(give)), (), size // 4, size)
        pieces = lax.all_to_all(pieces, "tm", 0, 0, axis_index_groups=groups)
        terms = lax.axis_size("tm") - 1
        (pieces,) = kernel_call(
            lambda *refs: sum_kernel(terms, *refs), [spread], (pieces,), (), size // 4, size
        )
        pieces = lax.all_to_all(pieces, "tm", 0, 0, axis_index_groups=groups)
        gradient_mine = pieces.reshape(strip)
        (gradient,) = kernel_call(
            whole_kernel, [square], (gradient_mine, swap_cores(gradient_mine)), (), size // 4, 2 * size
        )
    return covariance[None], gradient


def solution(mesh):
    return jax.shard_map(
        on_device,
        mesh=mesh,
        in_specs=(P(("rep", "tm"), None, None), P(("rep", "tm"), None, None), P("rep", None)),
        out_specs=(P(("rep", "tm"), None, None), P("rep", None)),
        check_vma=False,
    )
```
